32 devices in a mesh: dp: 2 (over x), seq: 4 (over y, core), tensor: 4 (over z).
Axes of the slice: x: 2, y: 2, z: 4, core: 2. Of those that a mesh axis runs over, the one named last changes fastest.
Arguments:
- frames: bfloat16 [4, 1024, 1536], P('dp', ('seq', 'tensor')), may hold values from -6 to 6
- text_states: bfloat16 [4, 64, 1536], P('dp'), may hold values from -6 to 6
- cotangent: bfloat16 [4, 1024, 1536], P('dp', ('seq', 'tensor')), may hold values from -6 to 6
- self_project: float32 [1536, 4608], P(('dp', 'seq'), 'tensor'), may hold values from -0.15625 to 0.15625
- self_merger: float32 [1536, 1536], P(('dp', 'seq'), 'tensor'), may hold values from -0.875 to 0.875
- cross_query: float32 [1536, 1536], P(('dp', 'seq'), 'tensor'), may hold values from -0.15625 to 0.15625
- cross_memory: float32 [1536, 3072], P(('dp', 'seq'), 'tensor'), may hold values from -0.15625 to 0.15625
- cross_blender: float32 [1536, 1536], P(('dp', 'seq'), 'tensor'), may hold values from -1.25 to 1.25
- feed_expand: float32 [1536, 6144], P(('dp', 'seq'), 'tensor'), may hold values from -0.15625 to 0.15625
- feed_reduce: float32 [1536, 6144], P(('dp', 'seq'), 'tensor'), may hold values from -0.078125 to 0.078125
- norm_gains: float32 [1536, 3], P(('dp', 'seq')), may hold values from 0.5 to 1.5
- norm_shifts: float32 [1536, 3], P(('dp', 'seq')), may hold values from -1 to 1
Outputs:
- layer_output: bfloat16 [4, 1024, 1536], P('dp', ('seq', 'tensor'))
- frames_grad: float32 [4, 1024, 1536], P('dp', ('seq', 'tensor'))
- text_grad: float32 [4, 64, 1536], P('dp', 'seq', 'tensor')
- project_grad: float32 [1536, 4608], P(('dp', 'seq'), 'tensor')
- merger_grad: float32 [1536, 1536], P(('dp', 'seq'), 'tensor')
- query_grad: float32 [1536, 1536], P(('dp', 'seq'), 'tensor')
- memory_grad: float32 [1536, 3072], P(('dp', 'seq'), 'tensor')
- blender_grad: float32 [1536, 1536], P(('dp', 'seq'), 'tensor')
- expand_grad: float32 [1536, 6144], P(('dp', 'seq'), 'tensor')
- reduce_grad: float32 [1536, 6144], P(('dp', 'seq'), 'tensor')
- gains_grad: float32 [1536, 3], P(('dp', 'seq'))
- shifts_grad: float32 [1536, 3], P(('dp', 'seq'))
The draws below stay inside these ranges and needn't reach their ends.
All inputs are finite; a program needn't handle non-finite values.
Results may differ from the reference program's by a relative error of at most 0.02.
The reference program's roundings to bfloat16 on the way count: a program that leaves them out, or rounds other values in their place, can miss the bound.
Values may be sent and summed in bfloat16 or wider, within the bound.
No kernel may reach another device: no remote copies, remote signals or barrier semaphores. Data moves between devices by JAX's collectives and lax.ppermute only.
A program may use at most 192 MiB of HBM per device.

```python
import math
from functools import partial
import jax
import jax.numpy as jnp
from jax import lax

D = 1536
HD = 64
FF = 6144
TEXT = 64
FRAMES = 1024
CLIPS = 4


def levels(own_key, extent, split, low, largest):
    loudness, own = 1.0, jax.random.fold_in(own_key, 6)
    for axis_at, shards_of in split:
        draws = jnp.exp(jax.random.uniform(jax.random.fold_in(own, axis_at), (shards_of,), jnp.float32, low / len(split), largest / len(split)))
        loudness = loudness * jnp.repeat(draws, extent[axis_at] // shards_of).reshape([-1 if axis == axis_at else 1 for axis in range(len(extent))])
    return loudness


def bell_draw(rng, extent, width, limit, cuts=(), held_as=jnp.bfloat16):
    level = levels(rng, extent, cuts, -0.22, 0.18) if cuts else 1.0
    values = jax.random.normal(rng, extent, jnp.float32) * width * level
    return jnp.minimum(jnp.maximum(values, -limit), limit).astype(held_as)


def setup_inputs(seed: int = 0) -> dict:
    arg_keys = jax.random.split(jax.random.key(seed), 13)
    frames = bell_draw(arg_keys[0], (CLIPS, FRAMES, D), 1.0, 6.0, ((0, 2), (1, 16)))
    text_states = bell_draw(arg_keys[1], (CLIPS, TEXT, D), 1.0, 6.0, ((0, 2),))
    cotangent = bell_draw(arg_keys[2], (CLIPS, FRAMES, D), 1.0, 6.0, ((0, 2), (1, 16)))
    self_project = bell_draw(arg_keys[3], (D, 3 * D), D ** -0.5, 0.15625, ((0, 8), (1, 4)), jnp.float32)
    self_merger = bell_draw(arg_keys[4], (D, D), (D // 32) ** -0.5, 0.875, ((0, 8), (1, 4)), jnp.float32)
    cross_query = bell_draw(arg_keys[5], (D, D), D ** -0.5, 0.15625, ((0, 8), (1, 4)), jnp.float32)
    cross_memory = bell_draw(arg_keys[6], (D, 2 * D), D ** -0.5, 0.15625, ((0, 8), (1, 4)), jnp.float32)
    cross_blender = bell_draw(arg_keys[7], (D, D), (D // 64) ** -0.5, 1.25, ((0, 8), (1, 4)), jnp.float32)
    feed_expand = bell_draw(arg_keys[8], (D, FF), D ** -0.5, 0.15625, ((0, 8), (1, 4)), jnp.float32)
    feed_reduce = bell_draw(arg_keys[9], (D, FF), FF ** -0.5, 0.078125, ((0, 8), (1, 4)), jnp.float32)
    norm_gains = jnp.clip(1.0 + 0.1 * jax.random.normal(arg_keys[10], (D, 3), jnp.float32), 0.5, 1.5)
    norm_shifts = bell_draw(arg_keys[11], (D, 3), 0.2, 1.0, ((0, 8),), jnp.float32)
    return dict(frames=frames, text_states=text_states, cotangent=cotangent, self_project=self_project, self_merger=self_merger, cross_query=cross_query, cross_memory=cross_memory, cross_blender=cross_blender, feed_expand=feed_expand, feed_reduce=feed_reduce, norm_gains=norm_gains, norm_shifts=norm_shifts)


@jax.custom_vjp
def low(v):
    return lax.optimization_barrier(v.astype(jnp.bfloat16)).astype(jnp.float32)

@jax.custom_vjp
def low_back(v):
    return v

def low_keep(v):
    return (low(v), None)

def low_pass(kept, grad):
    return (grad,)

def back_keep(v):
    return (v, None)

def back_low(kept, grad):
    return (low(grad),)
low.defvjp(low_keep, low_pass)
low_back.defvjp(back_keep, back_low)
norm_eps = 1e-05
masked_value = -1e+30
highest = lax.Precision.HIGHEST

def rounded_both(value):
    return low_back(low(value))

def product(left_side, right_side):
    return jnp.dot(left_side, right_side, precision=highest, preferred_element_type=jnp.float32)

def normalize(rows, gain, shift):
    row_mean = lax.optimization_barrier(jnp.mean(rows, axis=-1, keepdims=True))
    centred = rows - row_mean
    variance = lax.optimization_barrier(jnp.mean(centred * centred, axis=-1, keepdims=True))
    return centred * lax.rsqrt(variance + norm_eps) * gain + shift

def self_block(key_rows, value_rows, packed):
    query_rows, first_row = packed
    head_scale = HD ** (-0.5)
    raw_scores = jnp.einsum('qhd,khd->hqk', query_rows, key_rows, precision=highest) * head_scale
    scores = low_back(raw_scores)
    query_pos = first_row + jnp.arange(query_rows.shape[0], dtype=jnp.int32)
    key_pos = jnp.arange(key_rows.shape[0], dtype=jnp.int32)
    allowed = key_pos[None, :] <= query_pos[:, None]
    scores = jnp.where(allowed[None], scores, masked_value)
    soft_weights = low(jax.nn.softmax(scores, axis=-1))
    return jnp.einsum('hqk,khd->qhd', soft_weights, value_rows, precision=highest)

def decoder_layer(frames, text_states, self_project, self_merger, cross_query, cross_memory, cross_blender, feed_expand, feed_reduce, norm_gains, norm_shifts):
    self_project = low(self_project)
    self_merger = low(self_merger)
    cross_query = low(cross_query)
    cross_memory = low(cross_memory)
    cross_blender = low(cross_blender)
    feed_expand = low(feed_expand)
    feed_reduce = low(feed_reduce)
    gain_cols = low(norm_gains)
    shifts = low(norm_shifts)
    head_scale = HD ** (-0.5)
    head_count = self_project.shape[1] // (3 * HD)
    length = frames.shape[0]
    text_count = text_states.shape[0]
    block_rows = math.gcd(length, 512)
    count_blocks = length // block_rows
    normed = low(normalize(frames, gain_cols[:, 0], shifts[:, 0]))
    packed_qkv = rounded_both(product(normed, self_project)).reshape(length, head_count, 3, HD)
    queries = packed_qkv[:, :, 0]
    key_rows = packed_qkv[:, :, 1]
    value_rows = packed_qkv[:, :, 2]
    firsts = jnp.arange(count_blocks, dtype=jnp.int32) * block_rows
    attended = lax.map(jax.checkpoint(partial(self_block, key_rows, value_rows)), (queries.reshape(count_blocks, block_rows, head_count, HD), firsts))
    attended = rounded_both(attended.reshape(length, head_count * HD))
    first_res = frames + low_back(product(attended, self_merger.T))
    normed = low(normalize(first_res, gain_cols[:, 1], shifts[:, 1]))
    cross_rows = rounded_both(product(normed, cross_query)).reshape(length, head_count, HD)
    memory = rounded_both(product(text_states, cross_memory)).reshape(text_count, head_count, 2, HD)
    scores = low_back(jnp.einsum('qhd,khd->hqk', cross_rows, memory[:, :, 0], precision=highest) * head_scale)
    soft_weights = low(jax.nn.softmax(scores, axis=-1))
    mixed_rows = jnp.einsum('hqk,khd->qhd', soft_weights, memory[:, :, 1], precision=highest)
    mixed_rows = rounded_both(mixed_rows.reshape(length, head_count * HD))
    second_res = first_res + low_back(product(mixed_rows, cross_blender.T))
    normed = low(normalize(second_res, gain_cols[:, 2], shifts[:, 2]))
    hidden = low_back(product(normed, feed_expand))
    active = low(jax.nn.gelu(hidden, approximate=False))
    return second_res + low_back(product(active, feed_reduce.T))

def reference(frames, text_states, cotangent, self_project, self_merger, cross_query, cross_memory, cross_blender, feed_expand, feed_reduce, norm_gains, norm_shifts):
    masters = (self_project, self_merger, cross_query, cross_memory, cross_blender, feed_expand, feed_reduce, norm_gains, norm_shifts)

    def per_clip(totals, packed):
        clip_rows, text_rows, clip_cotangent = packed
        result, pullback = jax.vjp(decoder_layer, clip_rows.astype(jnp.float32), text_rows.astype(jnp.float32), *masters)
        gradients = pullback(clip_cotangent.astype(jnp.float32))
        totals = tuple((summed + fresh for summed, fresh in zip(totals, gradients[2:])))
        return (totals, (result.astype(jnp.bfloat16), gradients[0], gradients[1]))
    initial = tuple((jnp.zeros(master.shape, jnp.float32) for master in masters))
    totals, stacked = lax.scan(per_clip, initial, (frames, text_states, cotangent))
    return (stacked[0], stacked[1], stacked[2], totals[0], totals[1], totals[2], totals[3], totals[4], totals[5], totals[6], totals[7], totals[8])
```

```python
import jax
import jax.numpy as jnp
from jax import lax
from jax.sharding import PartitionSpec as P

HD = 64
norm_eps = 1e-05
masked_value = -1e30
bf16 = jnp.bfloat16
f32 = jnp.float32


def mm(a, b):
    return jnp.dot(a, b, preferred_element_type=f32)


def mm_nt(a, b):
    return lax.dot_general(a, b, (((1,), (1,)), ((), ())), preferred_element_type=f32)


def mm_tn(a, b):
    return lax.dot_general(a, b, (((0,), (0,)), ((), ())), preferred_element_type=f32)


def swap(v, axis, bit):
    n = lax.axis_size(axis)
    return lax.ppermute(v, axis, [(i, i ^ bit) for i in range(n)])


def cat(parts, axis=0):
    return parts[0] if len(parts) == 1 else jnp.concatenate(parts, axis=axis)


def norm_stats(v):
    centred = v - jnp.mean(v, axis=-1, keepdims=True)
    rstd = lax.rsqrt(jnp.mean(centred * centred, axis=-1, keepdims=True) + norm_eps)
    return centred * rstd, rstd


def normalize(v, gain, shift):
    return (norm_stats(v)[0] * gain + shift).astype(bf16)


def norm_backward(v, gain, dh):
    n, rstd = norm_stats(v)
    u = dh * gain
    dv = rstd * (
        u - jnp.mean(u, axis=-1, keepdims=True) - n * jnp.mean(u * n, axis=-1, keepdims=True)
    )
    return dv, jnp.sum(dh * n, axis=0), jnp.sum(dh, axis=0)


def gelu(z):
    return z * (1.0 + lax.erf(z * (0.5**0.5))) * 0.5


def gelu_slope(z):
    cdf = 0.5 * (1.0 + lax.erf(z * (0.5**0.5)))
    return cdf + z * jnp.exp(-0.5 * z * z) * (0.5 / jnp.pi) ** 0.5


class Blocks:
    def __init__(self):
        dp_size = lax.axis_size("dp")
        self.bits = [("seq", 2)]
        step = 1
        while step < dp_size:
            self.bits.append(("dp", step))
            step *= 2
        self.count = 2 ** len(self.bits)
        self.index = lax.axis_index("dp") * 2 + lax.axis_index("seq") // 2
        every = list(range(len(self.bits)))
        self.far_first = every[1:] + every[:1]
        self.near_first = every

    def flip(self, v, bit, axis=-1):
        axis = axis % v.ndim
        size = v.shape[axis] // self.count
        order = [j ^ (1 << bit) for j in range(self.count)]
        parts = [lax.slice_in_dim(v, j * size, (j + 1) * size, axis=axis) for j in order]
        return cat(parts, axis)

    def relative(self, v, axis=-1):
        for bit in range(len(self.bits)):
            v = jnp.where((self.index >> bit) & 1 == 1, self.flip(v, bit, axis), v)
        return v

    def gather(self, v, order, axis=0):
        held = {0: v}
        for bit in order:
            name, step = self.bits[bit]
            keys = sorted(held)
            got = swap(cat([held[k] for k in keys], axis), name, step)
            size = got.shape[axis] // len(keys)
            for i, k in enumerate(keys):
                held[k | (1 << bit)] = lax.slice_in_dim(got, i * size, (i + 1) * size, axis=axis)
        return cat([held[k] for k in range(self.count)], axis)

    def scatter(self, v, order, axis=0, wire=bf16):
        size = v.shape[axis] // self.count
        held = {
            j: lax.slice_in_dim(v, j * size, (j + 1) * size, axis=axis) for j in range(self.count)
        }
        for bit in order:
            name, step = self.bits[bit]
            keep = [k for k in sorted(held) if not k & (1 << bit)]
            sent = cat([held.pop(k | (1 << bit)) for k in keep], axis).astype(wire)
            got = swap(sent, name, step)
            for i, k in enumerate(keep):
                piece = lax.slice_in_dim(got, i * size, (i + 1) * size, axis=axis)
                held[k] = held[k].astype(f32) + piece.astype(f32)
        return held[0]


def shards(
    frames,
    text_states,
    cotangent,
    self_project,
    self_merger,
    cross_query,
    cross_memory,
    cross_blender,
    feed_expand,
    feed_reduce,
    norm_gains,
    norm_shifts,
):
    blocks = Blocks()
    clips, rows, width = frames.shape
    own = clips * rows
    head_scale = HD ** (-0.5)
    seq = lax.axis_index("seq")
    z = lax.axis_index("tensor")
    sh, sl = seq // 2, seq % 2
    text_count = text_states.shape[1]

    def by_clip(v):
        return jnp.where(sh == 0, v, v[::-1])

    def core_half(w):
        half = w.shape[1] // 2
        low, high = w[:, :half].astype(bf16), w[:, half:].astype(bf16)
        return jnp.where(sl == 0, low, high), jnp.where(sl == 0, high, low)

    def core_rows(shards_in):
        pairs = [core_half(w) for w in shards_in]
        kept = cat([p[0] for p in pairs], 1)
        got = swap(cat([p[1] for p in pairs], 1), "seq", 1)
        return jnp.where(sl == 0, cat([kept, got]), cat([got, kept]))

    def split_cols(v, shards_in):
        out, first = [], 0
        for w in shards_in:
            half = w.shape[1] // 2
            out.append(v[:, first : first + half])
            first += half
        return out

    def fetch(shards_in):
        near = core_rows(shards_in)
        far = swap(near, "tensor", 2)
        near = blocks.gather(near, blocks.far_first)
        far = blocks.gather(far, blocks.near_first)
        return list(zip(split_cols(near, shards_in), split_cols(far, shards_in)))

    def core_return(v, widths):
        half_rows = v.shape[0] // 2
        low, high = v[:half_rows], v[half_rows:]
        kept = jnp.where(sl == 0, low, high)
        got = swap(jnp.where(sl == 0, high, low).astype(bf16), "seq", 1).astype(f32)
        out, first = [], 0
        for half in widths:
            a, b = kept[:, first : first + half], got[:, first : first + half]
            out.append(jnp.where(sl == 0, cat([a, b], 1), cat([b, a], 1)))
            first += half
        return out

    def give(grads):
        near = cat([g[0] for g in grads], 1)
        far = cat([g[1] for g in grads], 1)
        far = blocks.scatter(far, blocks.far_first)
        near = blocks.scatter(near, blocks.near_first)
        near = near + swap(far.astype(bf16), "tensor", 2).astype(f32)
        return core_return(near, [g[0].shape[1] for g in grads])

    def row_gather(v):
        v = cat([v, swap(v, "tensor", 1)])
        return cat([v, swap(v, "seq", 1)])

    def row_scatter(v):
        half = v.shape[0] // 2
        v = v[:half] + swap(v[half:].astype(bf16), "seq", 1).astype(f32)
        half = half // 2
        return v[:half] + swap(v[half:].astype(bf16), "tensor", 1).astype(f32)

    def up(v, first):
        return lax.ppermute(v, "tensor", [(i, i + 1) for i in range(first, 3)])

    def down(v, first):
        return lax.ppermute(v, "tensor", [(3 - i, 2 - i) for i in range(first, 3)])

    def up_to(v, last):
        return lax.ppermute(v, "tensor", [(i, i + 1) for i in range(0, last)])

    def down_to(v, last):
        return lax.ppermute(v, "tensor", [(3 - i, 2 - i) for i in range(0, last)])

    def clip_gather(v):
        got = blocks.flip(swap(v[1], "seq", 2), 0)
        pair = jnp.stack([v[0], got])
        up_one, down_one = up(pair, 0), down(pair, 0)
        up_two, down_two = up(up_one, 1), down(down_one, 1)
        up_three, down_three = up(up_two, 2), down(down_two, 2)
        one = jnp.where(z % 2 == 1, up_one, down_one)
        two = jnp.where(z >= 2, up_two, down_two)
        three = jnp.where(
            z < 2,
            jnp.where(z == 0, down_three, down_one),
            jnp.where(z == 2, up_one, up_three),
        )
        line = jnp.stack([pair, one, two, three], axis=1)
        return jnp.stack([line, swap(line, "seq", 1)], axis=1)

    def clip_scatter(v):
        line = v[:, 0] + swap(v[:, 1].astype(bf16), "seq", 1).astype(f32)
        none, one, two, three = [line[:, j] for j in range(4)]
        up_sum = up_to(three.astype(bf16), 1).astype(f32)
        down_sum = down_to(three.astype(bf16), 1).astype(f32)
        up_sum = up_to((two + up_sum).astype(bf16), 2).astype(f32)
        down_sum = down_to((two + down_sum).astype(bf16), 2).astype(f32)
        up_sum = up_to((jnp.where(z == 1, three, one) + up_sum).astype(bf16), 3).astype(f32)
        down_sum = down_to((jnp.where(z == 2, three, one) + down_sum).astype(bf16), 3).astype(f32)
        pair = none + up_sum + down_sum
        got = blocks.flip(swap(pair[1].astype(bf16), "seq", 2), 0).astype(f32)
        return jnp.stack([pair[0], got])

    x_low = blocks.relative(by_clip(frames))
    clip_rows = clip_gather(x_low).reshape(16 * rows, width)
    x0 = x_low.reshape(own, width).astype(f32)
    g3_low = blocks.relative(by_clip(cotangent)).reshape(own, width)
    text = blocks.relative(by_clip(text_states)).reshape(clips * text_count, width)

    affine = cat([norm_gains.T, norm_shifts.T]).astype(bf16)
    other = swap(affine, "seq", 1)
    affine = jnp.where(sl == 0, cat([affine, other], 1), cat([other, affine], 1))
    affine = blocks.gather(affine, blocks.far_first, axis=1).astype(f32)
    gain, shift = affine[:3], affine[3:]

    project = blocks.gather(core_rows([self_project]), blocks.far_first)
    mids = [self_merger, cross_query, cross_memory, cross_blender]
    merger, query, memory, blender = fetch(mids)
    (expand,) = fetch([feed_expand])
    (reduce,) = fetch([feed_reduce])

    h1 = normalize(clip_rows.astype(f32), gain[0], shift[0])
    heads = project.shape[1] // (3 * HD)
    packed = mm(h1, project).astype(bf16).reshape(16 * rows, heads, 3, HD)
    q, k, v = packed[:, :, 0], packed[:, :, 1], packed[:, :, 2]
    own_block = sh * 8 + sl * 4 + z
    at = (own_block ^ jnp.arange(16, dtype=jnp.int32))[:, None] * rows
    at = (at + jnp.arange(rows, dtype=jnp.int32)[None, :]).reshape(-1)
    allowed = at[None, :] <= at[:, None]

    def self_weights():
        s = jnp.einsum("qhd,khd->hqk", q, k, preferred_element_type=f32) * head_scale
        return jax.nn.softmax(jnp.where(allowed, s, masked_value), axis=-1)

    a1f = self_weights()
    a1 = a1f.astype(bf16)
    o1 = jnp.einsum("hqk,khd->qhd", a1, v, preferred_element_type=f32).astype(bf16)
    o1 = o1.reshape(2, 2, 2, 2, rows, heads * HD)
    o1 = jnp.stack([o1[0], swap(o1[1], "seq", 2)])

    def tp_rows(v):
        return v.transpose(1, 2, 0, 3, 4).reshape(4 * own, heads * HD)

    o1_halves = (tp_rows(o1[:, :, 0]), tp_rows(swap(o1[:, :, 1], "tensor", 2)))
    x1 = x0 + row_scatter(mm_nt(o1_halves[0], merger[0]) + mm_nt(o1_halves[1], merger[1]))

    h2 = row_gather(normalize(x1, gain[1], shift[1]))
    mem = [mm(text, m).astype(bf16).reshape(clips, text_count, heads, 2, HD) for m in memory]

    def cross_forward(half):
        q2 = mm(h2, query[half]).astype(bf16).reshape(4, clips, rows, heads, HD)
        s = jnp.einsum(
            "acqhd,ckhd->chaqk", q2, mem[half][:, :, :, 0], preferred_element_type=f32
        )
        a2f = jax.nn.softmax(s * head_scale, axis=-1)
        a2 = a2f.astype(bf16)
        o2 = jnp.einsum(
            "chaqk,ckhd->acqhd", a2, mem[half][:, :, :, 1], preferred_element_type=f32
        )
        return q2, a2f, a2, o2.astype(bf16).reshape(4 * own, heads * HD)

    cross = [cross_forward(half) for half in range(2)]
    x2 = x1 + row_scatter(mm_nt(cross[0][3], blender[0]) + mm_nt(cross[1][3], blender[1]))

    h3 = row_gather(normalize(x2, gain[2], shift[2]))
    hidden = [mm(h3, e) for e in expand]
    active = [gelu(h).astype(bf16) for h in hidden]
    branch = row_scatter(mm_nt(active[0], reduce[0]) + mm_nt(active[1], reduce[1]))
    layer_output = (x2 + branch).astype(bf16).reshape(clips, rows, width)

    g3_rows = row_gather(g3_low)
    d_hidden = [(mm(g3_rows, r) * gelu_slope(h)).astype(bf16) for r, h in zip(reduce, hidden)]
    (reduce_grad,) = give([[mm_tn(g3_rows, a).astype(bf16) for a in active]])
    (expand_grad,) = give([[mm_tn(h3, d).astype(bf16) for d in d_hidden]])
    dh3 = row_scatter(mm_nt(d_hidden[0], expand[0]) + mm_nt(d_hidden[1], expand[1]))
    dx, gain_three, shift_three = norm_backward(x2, gain[2], dh3)
    g2 = g3_low.astype(f32) + dx

    gy2 = row_gather(g2.astype(bf16))

    def cross_backward(half):
        q2, a2f, a2, _ = cross[half]
        keys, values = mem[half][:, :, :, 0], mem[half][:, :, :, 1]
        do2 = mm(gy2, blender[half]).astype(bf16).reshape(4, clips, rows, heads, HD)
        da = jnp.einsum("acqhd,ckhd->chaqk", do2, values, preferred_element_type=f32)
        ds = (a2f * (da - jnp.sum(da * a2f, axis=-1, keepdims=True))).astype(bf16)
        dq = jnp.einsum("chaqk,ckhd->acqhd", ds, keys, preferred_element_type=f32) * head_scale
        dk = jnp.einsum("chaqk,acqhd->ckhd", ds, q2, preferred_element_type=f32) * head_scale
        dv = jnp.einsum("chaqk,acqhd->ckhd", a2, do2, preferred_element_type=f32)
        return dq.astype(bf16).reshape(4 * own, heads * HD), jnp.stack([dk, dv], axis=3)

    cross_grads = [cross_backward(half) for half in range(2)]
    dh2 = row_scatter(mm_nt(cross_grads[0][0], query[0]) + mm_nt(cross_grads[1][0], query[1]))
    blender_grad, query_grad = give(
        [
            [mm_tn(gy2, c[3]).astype(bf16) for c in cross],
            [mm_tn(h2, c[0]).astype(bf16) for c in cross_grads],
        ]
    )
    dx, gain_two, shift_two = norm_backward(x1, gain[1], dh2)
    g1 = g2 + dx

    d_mem = [c[1].reshape(clips * text_count, heads * 2 * HD) for c in cross_grads]
    d_own = d_mem[0] + swap(d_mem[1].astype(bf16), "tensor", 2).astype(f32)
    d_low = d_own.astype(bf16)
    d_pair = d_low.reshape(clips, text_count, -1)
    d_got = swap(d_pair, "seq", 2)[::-1]
    d_own = (d_own.reshape(d_pair.shape) + d_got.astype(f32)).astype(bf16)
    d_own = d_own.reshape(clips * text_count, heads * 2 * HD)
    size = width // blocks.count
    near = [j for j in range(blocks.count) if j % 2 == 0]
    text_near = cat([text[:, j * size : (j + 1) * size] for j in near], 1)
    mem_grad = mm_tn(text_near, d_own)
    held = {j: mem_grad[i * size : (i + 1) * size] for i, j in enumerate(near)}
    for bit in range(1, len(blocks.bits)):
        name, step = blocks.bits[bit]
        keep = [j for j in sorted(held) if not j & (1 << bit)]
        got = swap(cat([held.pop(j | (1 << bit)) for j in keep]).astype(bf16), name, step)
        for i, j in enumerate(keep):
            held[j] = held[j] + got[i * size : (i + 1) * size].astype(f32)
    (memory_grad,) = core_return(held[0], [held[0].shape[1]])

    part = text_count // 4
    dt = mm_nt(d_own, memory[0]).reshape(clips, 2, 2, part, width)
    dt = blocks.relative(jnp.where(sh == 0, dt[:, 0], dt[:, 1]))
    kept = jnp.where(sl == 0, dt[:, 0], dt[:, 1])
    sent = jnp.where(sl == 0, dt[:, 1], dt[:, 0]).astype(bf16)
    kept = kept + swap(sent, "seq", 1).astype(f32)
    for bit in (1, 0):
        half = kept.shape[-1] // 2
        low, high = kept[..., :half], kept[..., half:]
        mine = (z >> bit) & 1 == 0
        sent = jnp.where(mine, high, low).astype(bf16)
        kept = jnp.where(mine, low, high) + swap(sent, "tensor", 1 << bit).astype(f32)
    text_grad = by_clip(kept)

    gy1 = row_gather(g1.astype(bf16))
    do1 = [mm(gy1, m).astype(bf16) for m in merger]
    (merger_grad,) = give([[mm_tn(gy1, o).astype(bf16) for o in o1_halves]])

    def clip_rows_of(v):
        return v.reshape(2, 2, clips, rows, heads * HD).transpose(2, 0, 1, 3, 4)

    far = swap(clip_rows_of(do1[1]), "tensor", 2)
    do1 = jnp.stack([clip_rows_of(do1[0]), far], axis=2)
    do1 = jnp.stack([do1[0], swap(do1[1], "seq", 2)]).reshape(16 * rows, heads, HD)
    da = jnp.einsum("qhd,khd->hqk", do1, v, preferred_element_type=f32)
    ds = (a1f * (da - jnp.sum(da * a1f, axis=-1, keepdims=True))).astype(bf16)
    dq = jnp.einsum("hqk,khd->qhd", ds, k, preferred_element_type=f32) * head_scale
    dk = jnp.einsum("hqk,qhd->khd", ds, q, preferred_element_type=f32) * head_scale
    dv = jnp.einsum("hqk,qhd->khd", a1, do1, preferred_element_type=f32)
    d_packed = jnp.stack([dq, dk, dv], axis=2).astype(bf16).reshape(16 * rows, heads * 3 * HD)
    d_part = mm_nt(d_packed, project)
    dh1 = clip_scatter(d_part.reshape(2, 2, 4, rows, width)).reshape(own, width)
    project_grad = blocks.scatter(mm_tn(h1, d_packed).astype(bf16), blocks.near_first)
    (project_grad,) = core_return(project_grad, [project_grad.shape[1]])
    gain_one = jnp.sum(d_part * norm_stats(clip_rows.astype(f32))[0], axis=0)
    shift_one = jnp.sum(d_part, axis=0)
    dx = norm_backward(x0, gain[0], dh1)[0]
    frames_grad = (g1 + dx).reshape(clips, rows, width)

    sums = jnp.stack([gain_one, gain_two, gain_three, shift_one, shift_two, shift_three])
    sums = blocks.scatter(sums, blocks.near_first, axis=1, wire=f32)
    half = sums.shape[1] // 2
    low, high = sums[:, :half], sums[:, half:]
    sums = jnp.where(sl == 0, low, high) + swap(jnp.where(sl == 0, high, low), "seq", 1)
    sums = sums + swap(sums, "tensor", 1)
    sums = sums + swap(sums, "tensor", 2)

    return (
        by_clip(blocks.relative(layer_output)),
        by_clip(blocks.relative(frames_grad)),
        text_grad,
        project_grad,
        merger_grad,
        query_grad,
        memory_grad,
        blender_grad,
        expand_grad,
        reduce_grad,
        sums[:3].T,
        sums[3:].T,
    )


def solution(mesh):
    rows = P("dp", ("seq", "tensor"), None)
    weight = P(("dp", "seq"), "tensor")
    column = P(("dp", "seq"), None)
    in_specs = (rows, P("dp", None, None), rows) + (weight,) * 7 + (column,) * 2
    out_specs = (rows, rows, P("dp", "seq", "tensor")) + (weight,) * 7 + (column,) * 2
    return jax.shard_map(shards, mesh=mesh, in_specs=in_specs, out_specs=out_specs, check_vma=False)
```
